32 devices in a mesh: tok: 4 (over y, core), tp: 8 (over z, x).
Axes of the slice: x: 2, y: 2, z: 4, core: 2. Of those that a mesh axis runs over, the one named last changes fastest.
Arguments:
- residual: bfloat16 [1024, 16384], P('tok', 'tp')
- norm_gain: float32 [16384], replicated, may hold values from 0.5 to 1.5
- weight: bfloat16 [30720, 16384], P(('tok', 'tp')), may hold values from -6 to 6
- scale_codes: int32 [30720, 2], P(('tok', 'tp')), may hold values from 0 to 7
- zero_points: int32 [30720, 2], P(('tok', 'tp')), may hold values from 4 to 11
- panels: bfloat16 [256, 16384], P(None, ('tok', 'tp')), as said below
Outputs:
- gram: float32 [16384, 16384], P('tok', 'tp')
- quantized: bfloat16 [30720, 16384], P('tok', 'tp')
The draws below stay inside these ranges and needn't reach their ends.
Inputs may be any that keep to these rules, and one draw needn't show every extreme that they name: Row j of panels is row j of an upper-triangular factor: entries left of column j are zero and panels[j, j] lies in [0.5, 1.5].
All inputs are finite; a program needn't handle non-finite values.
Results may differ from the reference program's by a relative error of at most 0.0085.
Values may be sent and summed in bfloat16 or wider, within the bound.
A program may use at most 384 MiB of HBM per device.

```python
import math
import jax
import jax.numpy as jnp
from jax import lax

D = 16384
FF = 30720
TOK_DEV = 256
BLOCK = 128
BLOCKS = 2
TOKENS = 1024
N_TOK = 4


def draw_residual(key, part):
    key_cols, key_rows, key_base = jax.random.split(key, 3)
    place = jnp.arange(D, dtype=jnp.float32) / D
    col_scale = jnp.exp(math.log(10.0) * place + jax.random.uniform(key_cols, (D,), minval=-0.5, maxval=0.5))
    row_scale = jnp.exp(jax.random.uniform(key_rows, (TOKENS, 1), minval=0.0, maxval=math.log(10.0)))
    base = jax.random.normal(key_base, (TOKENS, D))
    return (base * col_scale[None, :] * row_scale).astype(jnp.bfloat16)


def draw_panels(key, part):
    key_off, key_diag = jax.random.split(key)
    row_ids = jnp.arange(BLOCKS * BLOCK, dtype=jnp.int32)[:, None]
    col_ids = jnp.arange(D, dtype=jnp.int32)[None, :]
    spread = 0.12 * jax.random.normal(key_off, (BLOCKS * BLOCK, D))
    pivots = jax.random.uniform(key_diag, (BLOCKS * BLOCK, 1), minval=0.5, maxval=1.5)
    values = jnp.where(col_ids > row_ids, spread, jnp.where(col_ids == row_ids, pivots, 0.0))
    return values.astype(jnp.bfloat16)


def set_ends(entries, key, smallest, top_value):
    extent = entries.shape
    spot = [jax.random.randint(jax.random.fold_in(key, axis), (), 0, extent[axis]) for axis in range(len(extent))]
    entries = entries.at[tuple(spot)].set(smallest)
    longest = extent.index(max(extent))
    spot[longest] = (spot[longest] + 1) % extent[longest]
    return entries.at[tuple(spot)].set(top_value)


def block_levels(own_key, dims, cuts, low, largest):
    gain, own = 1.0, jax.random.fold_in(own_key, 6)
    for axis_at, shards_of in cuts:
        draws = jnp.exp(jax.random.uniform(jax.random.fold_in(own, axis_at), (shards_of,), jnp.float32, low / len(cuts), largest / len(cuts)))
        gain = gain * jnp.repeat(draws, dims[axis_at] // shards_of).reshape([-1 if axis == axis_at else 1 for axis in range(len(dims))])
    return gain


def scatter_about(rng, extent, deviation, bound, cuts=(), kind=jnp.bfloat16):
    drawn = deviation * jax.random.normal(rng, extent, jnp.float32)
    if cuts:
        drawn = drawn * block_levels(rng, extent, cuts, -0.22, 0.18)
    return jnp.clip(drawn, -bound, bound).astype(kind)


def setup_inputs(seed: int = 0) -> dict:
    key_of = jax.random.split(jax.random.key(seed), 7)
    return {
        "residual": draw_residual(jax.random.fold_in(key_of[6], 71), 0),
        "norm_gain": jnp.clip(1.0 + 0.1 * jax.random.normal(key_of[1], (D,), jnp.float32), 0.5, 1.5),
        "weight": scatter_about(key_of[2], (FF, D), 1.0, 6.0, ((0, 32),)),
        "scale_codes": set_ends(jax.random.randint(key_of[3], (FF, BLOCKS), 0, 8), jax.random.fold_in(key_of[3], 1), 0, 7).astype(jnp.int32),
        "zero_points": set_ends(jax.random.randint(key_of[4], (FF, BLOCKS), 4, 12), jax.random.fold_in(key_of[4], 1), 4, 11).astype(jnp.int32),
        "panels": draw_panels(jax.random.fold_in(key_of[6], 71), 0),
    }


EPS = 1e-05
SOFTNESS = 0.9
FULL_TURN = 2.0 * math.pi

def dequantize(column, scale_row, zero_row):
    shifted = column / scale_row + zero_row
    softened = shifted - SOFTNESS * jnp.sin(FULL_TURN * shifted) / FULL_TURN
    return scale_row * (jnp.clip(softened, 0.0, 15.0) - zero_row)

def reference(residual, norm_gain, weight, scale_codes, zero_points, panels):
    resid_f = residual.astype(jnp.float32)
    mean_square = lax.optimization_barrier(jnp.mean(resid_f * resid_f, axis=1, keepdims=True))
    normed = (resid_f * lax.rsqrt(mean_square + EPS) * norm_gain[None, :]).astype(jnp.bfloat16)
    groups = normed.astype(jnp.float32).reshape(N_TOK, TOK_DEV, D)
    col_width = D // 16

    def gram_block(block_id):
        cols_first = block_id * col_width
        running = jnp.zeros((D, col_width), jnp.float32)
        for g in range(N_TOK):
            group_rows = groups[g]
            right_cols = lax.dynamic_slice_in_dim(group_rows, cols_first, col_width, 1)
            group_term = lax.dot_general(group_rows, right_cols, (((0,), (0,)), ((), ())), preferred_element_type=jnp.float32)
            rounded = lax.optimization_barrier(group_term.astype(jnp.bfloat16))
            running = running + rounded.astype(jnp.float32)
        return running / TOKENS
    blocks_out = lax.map(gram_block, jnp.arange(16, dtype=jnp.int32))
    gram = jnp.transpose(blocks_out, (1, 0, 2)).reshape(D, D)
    column = jnp.arange(D, dtype=jnp.int32)
    lane_ids = jnp.arange(BLOCK, dtype=jnp.int32)

    def quantize_rows(inputs):
        weight_rows, codes, zeros_in = inputs
        working = weight_rows.astype(jnp.float32)
        for k in range(BLOCKS):
            block_start = k * BLOCK
            scale_row = jnp.exp2(codes[:, k].astype(jnp.float32) * 0.5 - 3.0)
            zero_row = zeros_in[:, k].astype(jnp.float32)
            panel_rows = panels[block_start:block_start + BLOCK].astype(jnp.float32)
            diagonal = panel_rows[:, block_start:block_start + BLOCK]

            def column_step(block_cols, j):
                column_now = lax.dynamic_index_in_dim(block_cols, j, 1, keepdims=False)
                pivot_row = lax.dynamic_index_in_dim(diagonal, j, 0, keepdims=False)
                pivot = jnp.sum(jnp.where(lane_ids == j, pivot_row, 0.0))
                restored = dequantize(column_now, scale_row, zero_row)
                error_now = (column_now - restored) / pivot
                block_cols = block_cols - error_now[:, None] * jnp.where(lane_ids > j, pivot_row, 0.0)[None, :]
                block_cols = jnp.where((lane_ids == j)[None, :], restored[:, None], block_cols)
                return (block_cols, error_now)
            block_cols, errors = lax.scan(column_step, working[:, block_start:block_start + BLOCK], lane_ids)
            correction = jnp.dot(errors.T, panel_rows, precision=lax.Precision.HIGHEST)
            working = jnp.where((column >= block_start + BLOCK)[None, :], working - correction, working)
            working = working.at[:, block_start:block_start + BLOCK].set(block_cols)
        return working.astype(jnp.bfloat16)
    row_blocks = max(1, FF // 2048)
    stacked = lax.map(quantize_rows, (weight.reshape(row_blocks, FF // row_blocks, D), scale_codes.reshape(row_blocks, FF // row_blocks, BLOCKS), zero_points.reshape(row_blocks, FF // row_blocks, BLOCKS)))
    quantized = stacked.reshape(FF, D)
    return (gram, quantized)
```

```python
import math

import jax
import jax.numpy as jnp
from jax import lax
from jax.sharding import PartitionSpec as P


BLOCK = 128
BLOCKS = 2


EPS = 1e-05
SOFTNESS = 0.9
FULL_TURN = 2.0 * math.pi
HIGHEST = lax.Precision.HIGHEST


def dequantize(column, scale_row, zero_row):
    shifted = column / scale_row + zero_row
    softened = shifted - SOFTNESS * jnp.sin(FULL_TURN * shifted) / FULL_TURN
    return scale_row * (jnp.clip(softened, 0.0, 15.0) - zero_row)


def block_errors(block_cols, diagonal, scale_row, zero_row):
    row_count = block_cols.shape[0]
    block_width = block_cols.shape[1]
    lane_ids = lax.iota(jnp.int32, 8)
    wide_ids = lax.iota(jnp.int32, block_width)

    def sub_step(step_index, carried):
        block_now, errors = carried
        sub_first = step_index * 8
        sub_cols = lax.dynamic_slice_in_dim(block_now, sub_first, 8, 1)
        sub_panel = lax.dynamic_slice_in_dim(diagonal, sub_first, 8, 0)
        local_pivots = lax.dynamic_slice_in_dim(sub_panel, sub_first, 8, 1)
        collected = []
        for i in range(8):
            column_now = sub_cols[:, i]
            restored = dequantize(column_now, scale_row, zero_row)
            error_now = (column_now - restored) / local_pivots[i, i]
            sub_cols = (
                sub_cols
                - error_now[:, None] * jnp.where(lane_ids > i, local_pivots[i], 0.0)[None, :]
            )
            sub_cols = jnp.where((lane_ids == i)[None, :], restored[:, None], sub_cols)
            collected.append(error_now)
        sub_errors = jnp.stack(collected, axis=1)
        spill_over = jnp.dot(sub_errors, sub_panel, precision=HIGHEST)
        block_now = jnp.where(
            (wide_ids >= sub_first + 8)[None, :], block_now - spill_over, block_now
        )
        block_now = lax.dynamic_update_slice_in_dim(block_now, sub_cols, sub_first, 1)
        errors = lax.dynamic_update_slice_in_dim(errors, sub_errors, sub_first, 1)
        return (block_now, errors)

    start_state = (block_cols, jnp.zeros((row_count, block_width), jnp.float32))
    return lax.fori_loop(0, block_width // 8, sub_step, start_state)


def exchange(array, axis, step):
    count = lax.axis_size(axis)
    return lax.ppermute(array, axis, [(i, i ^ step) for i in range(count)])


def far_first(count):
    return sorted(range(1, count), reverse=True)


def panel_columns(panels):
    tok_count = lax.axis_size("tok")
    tp_count = lax.axis_size("tp")
    tok_place = lax.axis_index("tok")
    pieces = []
    for r in range(tok_count):
        pairs = []
        for t in range(tok_count):
            for p in range(tp_count):
                source = tok_count * p + (t + r) % tok_count
                pairs.append((source, t * tp_count + p))
        pieces.append(lax.ppermute(panels, ("tok", "tp"), pairs))
    stacked = jnp.stack(pieces)
    ordered = [
        lax.dynamic_index_in_dim(stacked, (i - tok_place) % tok_count, 0, keepdims=False)
        for i in range(tok_count)
    ]
    return jnp.concatenate(ordered, axis=1)


def on_device(residual, norm_gain, weight, scale_codes, zero_points, panels):
    tok_local, feat_local = residual.shape
    tp_count = lax.axis_size("tp")
    tok_count = lax.axis_size("tok")
    feat_total = feat_local * tp_count
    tp_place = lax.axis_index("tp")
    tok_place = lax.axis_index("tok")
    row_count = weight.shape[0]

    def columns_of(place):
        return lax.dynamic_slice_in_dim(weight, place * feat_local, feat_local, 1)

    chunks = {}
    for s in far_first(tp_count):
        chunks[s] = exchange(columns_of(tp_place ^ s), "tp", s)
    chunks[0] = columns_of(tp_place)

    shard_cols = panels.shape[1]
    corner_parts = []
    for k in range(BLOCKS):
        root_index = k * BLOCK // shard_cols
        offset_cols = k * BLOCK - root_index * shard_cols
        corner_parts.append(
            jnp.where(
                lax.axis_index(("tok", "tp")) == root_index,
                panels[:, offset_cols : offset_cols + BLOCK],
                0,
            )
        )
    corner = lax.psum(jnp.concatenate(corner_parts, axis=1), ("tok", "tp")).astype(jnp.float32)

    local_rows = residual.astype(jnp.float32)
    row_sums = lax.psum(jnp.sum(local_rows * local_rows, axis=1), "tp")
    gain_own = lax.dynamic_slice_in_dim(norm_gain, tp_place * feat_local, feat_local, 0)
    x_own = (
        local_rows * lax.rsqrt(row_sums[:, None] / feat_total + EPS) * gain_own[None, :]
    ).astype(jnp.bfloat16)
    working = weight[:, : BLOCKS * BLOCK].astype(jnp.float32)
    working, x_own = lax.optimization_barrier((working, x_own))
    x_full = lax.all_gather(x_own, "tp", axis=1, tiled=True)
    all_errors = []
    for k in range(BLOCKS):
        if k == 1:
            all_errors[0], x_full = lax.optimization_barrier((all_errors[0], x_full))
        first = k * BLOCK
        scale_row = jnp.exp2(scale_codes[:, k].astype(jnp.float32) * 0.5 - 3.0)
        zero_row = zero_points[:, k].astype(jnp.float32)
        block_cols = working[:, first : first + BLOCK]
        for before in range(k):
            block_cols = block_cols - jnp.dot(
                all_errors[before],
                corner[before * BLOCK : (before + 1) * BLOCK, first : first + BLOCK],
                precision=HIGHEST,
            )
        _, errors = block_errors(
            block_cols, corner[first : first + BLOCK, first : first + BLOCK], scale_row, zero_row
        )
        all_errors.append(errors)
    own_errors = jnp.concatenate(all_errors, axis=1).astype(jnp.bfloat16)
    errors_of = lax.all_gather(own_errors, "tp", axis=0)
    own_panels = panel_columns(panels)

    gram_rows = feat_total // tok_count
    left, right = [], []
    for s in range(tok_count):
        slab = lax.dynamic_slice_in_dim(x_full, (tok_place ^ s) * gram_rows, gram_rows, 1)
        left.append(exchange(slab, "tok", s) if s else slab)
        right.append(exchange(x_own, "tok", s) if s else x_own)
    gram = lax.dot_general(
        jnp.concatenate(left, axis=0),
        jnp.concatenate(right, axis=0),
        (((0,), (0,)), ((), ())),
        preferred_element_type=jnp.float32,
    ) / (tok_local * tok_count)

    quantized = jnp.zeros((row_count * tp_count, feat_local), jnp.bfloat16)
    for s in sorted(range(tp_count), key=lambda s: (s != 0, s)):
        source = tp_place ^ s
        moved = jnp.dot(
            lax.dynamic_index_in_dim(errors_of, source, 0, keepdims=False),
            own_panels,
            preferred_element_type=jnp.float32,
        )
        rows_now = (chunks[s].astype(jnp.float32) - moved).astype(jnp.bfloat16)
        quantized = lax.dynamic_update_slice_in_dim(quantized, rows_now, source * row_count, 0)
    return (gram, quantized)


def solution(mesh):
    in_specs = (
        P("tok", "tp"),
        P(),
        P(("tok", "tp"), None),
        P(("tok", "tp"), None),
        P(("tok", "tp"), None),
        P(None, ("tok", "tp")),
    )
    out_specs = (P("tok", "tp"), P("tok", "tp"))

    return jax.shard_map(on_device, mesh=mesh, in_specs=in_specs, out_specs=out_specs, check_vma=False)
```
